256 devices in a mesh: rows: 128 (over y, x, z_hi, core), batch: 2 (over z_lo).
Axes of the slice: x: 4, y: 4, z: 8 (z_hi: 4, z_lo: 2; z = z_hi * 2 + z_lo), core: 2. Of those that a mesh axis runs over, the one named last changes fastest.
Arguments:
- features: bfloat16 [2, 512, 512, 128], P('batch', 'rows'), may hold values from -64 to 64
- grad_out: bfloat16 [2, 512, 512, 128], P('batch', 'rows'), may hold values from -6 to 6
- qkv_weight: bfloat16 [128, 384], replicated, may hold values from -8 to 8
- proj_weight: bfloat16 [128, 128], replicated, may hold values from -0.5 to 0.5
- lepe_weight: bfloat16 [9, 128], replicated, may hold values from -2 to 2
Outputs:
- grad_features: bfloat16 [2, 512, 512, 128], P('batch', 'rows')
- grad_qkv: float32 [128, 384], replicated
- grad_proj: float32 [128, 128], replicated
- grad_lepe: float32 [9, 128], replicated
The draws below stay inside these ranges and needn't reach their ends.
All inputs are finite; a program needn't handle non-finite values.
Results may differ from the reference program's by a relative error of at most 0.0055.
The reference program's roundings to bfloat16 on the way count: a program that leaves them out, or rounds other values in their place, can miss the bound.
Values may be sent and summed in bfloat16 or wider, within the bound.
A program may use at most 64 MiB of HBM per device.

```python
import math
import jax
import jax.numpy as jnp
from jax import lax

CHANNELS = 128
NUM_HEADS = 4
STRIPE = 2
MAP_ROWS = 512
MAP_COLS = 512
TILE_COUNT = 2


def draw_features(key, part):
    shape = (TILE_COUNT, MAP_ROWS, MAP_COLS, CHANNELS)
    base = jax.random.truncated_normal(jax.random.fold_in(key, 11), -6.0, 6.0, shape, jnp.float32)
    return base.astype(jnp.bfloat16)


def draw_qkv_weight(key, part):
    shape = (CHANNELS, 3 * CHANNELS)
    base = jax.random.truncated_normal(jax.random.fold_in(key, 21), -6.0, 6.0, shape, jnp.float32) * CHANNELS ** (-0.5)
    return base.astype(jnp.bfloat16)


def block_scale(rng, dims, cuts, low, largest):
    gain = 1.0
    for dim, parts in cuts:
        steps = jax.random.uniform(jax.random.fold_in(jax.random.fold_in(rng, 6), dim), (parts,), jnp.float32, low / len(cuts), largest / len(cuts))
        gain = gain * jnp.repeat(jnp.exp(steps), dims[dim] // parts).reshape((-1,) + (1,) * (len(dims) - 1 - dim))
    return gain


def normal_values(key, shape, scale, limit, cuts=(), held_as=jnp.bfloat16):
    factor_of = block_scale(key, shape, cuts, -0.22, 0.18) if cuts else 1.0
    values = jax.random.normal(key, shape, jnp.float32) * scale * factor_of
    return jnp.minimum(jnp.maximum(values, -limit), limit).astype(held_as)


def setup_inputs(seed: int = 0) -> dict:
    key_of = jax.random.split(jax.random.key(seed), 6)
    features = draw_features(jax.random.fold_in(key_of[5], 71), 0)
    grad_out = normal_values(key_of[1], (TILE_COUNT, MAP_ROWS, MAP_COLS, CHANNELS), 1.0, 6.0, ((0, 2), (1, 128)))
    qkv_weight = draw_qkv_weight(jax.random.fold_in(key_of[5], 71), 0)
    proj_weight = normal_values(key_of[3], (CHANNELS, CHANNELS), CHANNELS ** -0.5, 0.5)
    lepe_weight = normal_values(key_of[4], (9, CHANNELS), 9 ** -0.5, 2.0)
    return {"features": features, "grad_out": grad_out, "qkv_weight": qkv_weight, "proj_weight": proj_weight, "lepe_weight": lepe_weight}


EPSILON = 1e-05

def stripe_head(queries, key_rows, values, grad_rows):
    length = queries.shape[0]
    head_size = queries.shape[1]
    block_rows = math.gcd(length, 512)
    block_count = length // block_rows
    score_scale = head_size ** (-0.5)
    query_blocks = queries.reshape(block_count, block_rows, head_size)
    grad_blocks = grad_rows.reshape(block_count, block_rows, head_size)

    def advance(carry, pieces):
        key_grad, value_grad = carry
        query_block, grad_block = pieces
        scores = jnp.dot(query_block, key_rows.T, preferred_element_type=jnp.float32) * score_scale
        row_max = lax.optimization_barrier(jnp.max(scores, axis=1, keepdims=True))
        raised = jnp.exp(scores - row_max)
        probs_full = raised / lax.optimization_barrier(jnp.sum(raised, axis=1, keepdims=True))
        probs_low = probs_full.astype(jnp.bfloat16)
        out_block = jnp.dot(probs_low, values, preferred_element_type=jnp.float32)
        grad_probs = jnp.dot(grad_block, values.T, preferred_element_type=jnp.float32)
        row_inner = lax.optimization_barrier(jnp.sum(probs_full * grad_probs, axis=1, keepdims=True))
        grad_scores = (probs_full * (grad_probs - row_inner) * score_scale).astype(jnp.bfloat16)
        query_grad = jnp.dot(grad_scores, key_rows, preferred_element_type=jnp.float32)
        key_grad = key_grad + jnp.dot(grad_scores.T, query_block, preferred_element_type=jnp.float32)
        value_grad = value_grad + jnp.dot(probs_low.T, grad_block, preferred_element_type=jnp.float32)
        return ((key_grad, value_grad), (out_block, query_grad))
    zeros_init = jnp.zeros((length, head_size), jnp.float32)
    (key_grad, value_grad), (out_blocks, query_grads) = lax.scan(advance, (zeros_init, zeros_init), (query_blocks, grad_blocks))
    return (out_blocks.reshape(length, head_size), query_grads.reshape(length, head_size), key_grad, value_grad)

def stripes_backward(qkv_rows, grad_rows, head_size):
    group_count, length, triple = qkv_rows.shape
    half_width = triple // 3
    heads_here = half_width // head_size

    def split_heads(packed):
        return packed.reshape(group_count, length, heads_here, head_size).transpose(0, 2, 1, 3).reshape(group_count * heads_here, length, head_size)

    def merge_heads(items):
        return items.reshape(group_count, heads_here, length, head_size).transpose(0, 2, 1, 3).reshape(group_count, length, half_width)
    pieces = (split_heads(qkv_rows[:, :, :half_width]), split_heads(qkv_rows[:, :, half_width:2 * half_width]), split_heads(qkv_rows[:, :, 2 * half_width:]), split_heads(grad_rows))
    results = lax.map(lambda item_parts: stripe_head(*item_parts), pieces)
    return tuple((merge_heads(result) for result in results))

def lepe_terms(values_pad, grad_pad, weights, row_axis, col_axis):
    row_count = values_pad.shape[row_axis] - 2
    col_count = values_pad.shape[col_axis] - 2

    def window(source, row_off, col_off):
        sliced = lax.slice_in_dim(source, 1 + row_off, 1 + row_off + row_count, axis=row_axis)
        return lax.slice_in_dim(sliced, 1 + col_off, 1 + col_off + col_count, axis=col_axis)
    values_wide = values_pad.astype(jnp.float32)
    grad_wide = grad_pad.astype(jnp.float32)
    centre = window(grad_wide, 0, 0)
    summed_axes = tuple(range(values_pad.ndim - 1))
    lepe_out = jnp.zeros(centre.shape, jnp.float32)
    grad_values = jnp.zeros(centre.shape, jnp.float32)
    grad_list = []
    for row_off in (-1, 0, 1):
        for col_off in (-1, 0, 1):
            tap_weight = weights[(row_off + 1) * 3 + col_off + 1]
            shifted = window(values_wide, row_off, col_off)
            lepe_out = lepe_out + tap_weight * shifted
            grad_values = grad_values + tap_weight * window(grad_wide, -row_off, -col_off)
            grad_list.append(lax.optimization_barrier(jnp.sum(centre * shifted, axis=summed_axes)))
    return (lepe_out, grad_values, jnp.stack(grad_list))

def tile_backward(features, grad_out, qkv_weight, proj_weight, lepe_weight):
    map_rows, map_cols, channels = features.shape
    half_width = channels // 2
    head_size = channels // NUM_HEADS
    tokens_flat = features.reshape(-1, channels).astype(jnp.float32)
    centred = tokens_flat - lax.optimization_barrier(jnp.mean(tokens_flat, axis=1, keepdims=True))
    inv_std = lax.rsqrt(lax.optimization_barrier(jnp.mean(centred * centred, axis=1, keepdims=True)) + EPSILON)
    unit_norm = centred * inv_std
    normed = unit_norm.astype(jnp.bfloat16)
    w_horiz = jnp.concatenate([qkv_weight[:, 0:half_width], qkv_weight[:, channels:channels + half_width], qkv_weight[:, 2 * channels:2 * channels + half_width]], axis=1)
    w_vert = jnp.concatenate([qkv_weight[:, half_width:channels], qkv_weight[:, channels + half_width:2 * channels], qkv_weight[:, 2 * channels + half_width:]], axis=1)
    qkv_horiz = jnp.dot(normed, w_horiz, preferred_element_type=jnp.float32).astype(jnp.bfloat16)
    qkv_vert = jnp.dot(normed, w_vert, preferred_element_type=jnp.float32).astype(jnp.bfloat16)
    grad_flat = grad_out.reshape(-1, channels)
    grad_attn = jnp.dot(grad_flat, proj_weight.T, preferred_element_type=jnp.float32).astype(jnp.bfloat16)
    weights_wide = lepe_weight.astype(jnp.float32)
    pad_window = ((0, 0), (1, 1), (1, 1), (0, 0))
    group_count = map_rows // STRIPE
    length = STRIPE * map_cols
    attn_h, query_h, key_h, value_h = stripes_backward(qkv_horiz.reshape(group_count, length, 3 * half_width), grad_attn[:, :half_width].reshape(group_count, length, half_width), head_size)
    window_shape = (group_count, STRIPE, map_cols, half_width)
    lepe_h, lepe_grad_h, tap_grad_h = lepe_terms(jnp.pad(qkv_horiz[:, 2 * half_width:].reshape(window_shape), pad_window), jnp.pad(grad_attn[:, :half_width].reshape(window_shape), pad_window), weights_wide[:, :half_width], 1, 2)
    col_groups = map_cols // STRIPE
    col_length = map_rows * STRIPE

    def columns(source):
        return source.reshape(map_rows, col_groups, STRIPE, source.shape[-1]).transpose(1, 0, 2, 3)

    def rows_back(source):
        return source.transpose(1, 0, 2, 3).reshape(map_rows * map_cols, source.shape[-1])

    def flat_rows(source):
        return source.reshape(map_rows * map_cols, half_width)
    qkv_cols = columns(qkv_vert)
    grad_cols = columns(grad_attn[:, half_width:])
    attn_v, query_v, key_v, value_v = stripes_backward(qkv_cols.reshape(col_groups, col_length, 3 * half_width), grad_cols.reshape(col_groups, col_length, half_width), head_size)
    lepe_v, lepe_grad_v, tap_grad_v = lepe_terms(jnp.pad(qkv_cols[..., 2 * half_width:], pad_window), jnp.pad(grad_cols, pad_window), weights_wide[:, half_width:], 1, 2)
    col_shape = (col_groups, map_rows, STRIPE, half_width)
    attn = jnp.concatenate([flat_rows(attn_h) + flat_rows(lepe_h), rows_back(attn_v.reshape(col_shape) + lepe_v)], axis=1).astype(jnp.bfloat16)
    grad_tokens = jnp.concatenate([flat_rows(query_h), rows_back(query_v.reshape(col_shape)), flat_rows(key_h), rows_back(key_v.reshape(col_shape)), flat_rows(value_h) + flat_rows(lepe_grad_h), rows_back(value_v.reshape(col_shape) + lepe_grad_v)], axis=1).astype(jnp.bfloat16)
    grad_proj_part = jnp.dot(attn.T, grad_flat, preferred_element_type=jnp.float32)
    grad_qkv_part = jnp.dot(normed.T, grad_tokens, preferred_element_type=jnp.float32)
    grad_unit = jnp.dot(grad_tokens, qkv_weight.T, preferred_element_type=jnp.float32)
    grad_norm = (grad_unit - lax.optimization_barrier(jnp.mean(grad_unit, axis=1, keepdims=True)) - unit_norm * lax.optimization_barrier(jnp.mean(grad_unit * unit_norm, axis=1, keepdims=True))) * inv_std
    grad_features = (grad_flat.astype(jnp.float32) + grad_norm).astype(jnp.bfloat16).reshape(map_rows, map_cols, channels)
    tap_total = jnp.concatenate([tap_grad_h, tap_grad_v], axis=1)
    return (grad_features, grad_qkv_part, grad_proj_part, tap_total)

def reference(features, grad_out, qkv_weight, proj_weight, lepe_weight):
    grad_list = []
    grad_qkv = jnp.zeros((CHANNELS, 3 * CHANNELS), jnp.float32)
    grad_proj = jnp.zeros((CHANNELS, CHANNELS), jnp.float32)
    grad_lepe = jnp.zeros((9, CHANNELS), jnp.float32)
    for tile in range(TILE_COUNT):
        tile_grad, qkv_part, proj_part, tap_part = tile_backward(features[tile], grad_out[tile], qkv_weight, proj_weight, lepe_weight)
        grad_list.append(tile_grad)
        grad_qkv = grad_qkv + qkv_part
        grad_proj = grad_proj + proj_part
        grad_lepe = grad_lepe + tap_part
    grad_scale = (TILE_COUNT * MAP_ROWS * MAP_COLS) ** (-0.5)
    return (jnp.stack(grad_list), grad_qkv * grad_scale, grad_proj * grad_scale, grad_lepe * grad_scale)
```

```python
import functools

import jax
import jax.numpy as jnp
from jax import lax
from jax.experimental import pallas as pl
from jax.experimental.pallas import tpu as pltpu
from jax.sharding import PartitionSpec as P

NUM_HEADS = 4
STRIPE = 2
EPSILON = 1e-05
LOG2E = 1.4426950408889634
CONTRACT_COLS = (((1,), (1,)), ((), ()))
CONTRACT_ROWS = (((0,), (0,)), ((), ()))
MESH = pl.DeviceIdType.MESH
QUERY_BLOCK = 512


def dot(left, right, dims=(((1,), (0,)), ((), ()))):
    return lax.dot_general(left, right, dims, preferred_element_type=jnp.float32)


def normalise(tokens):
    centred = tokens - jnp.mean(tokens, axis=1, keepdims=True)
    inv_std = lax.rsqrt(jnp.mean(centred * centred, axis=1, keepdims=True) + EPSILON)
    return centred * inv_std, inv_std


def attention(nat, tra, outs, length, heads, size):
    out_ref, dq_ref, dk_ref, dv_ref = outs
    half = heads * size
    scale = size ** (-0.5)
    block = QUERY_BLOCK
    for step in range(length // block):
        rows = slice(step * block, (step + 1) * block)
        for head in range(heads):
            cols = [slice(part * half + head * size, part * half + (head + 1) * size) for part in range(4)]
            mine = slice(head * size, (head + 1) * size)
            k_tra = tra[cols[1], :]
            v_tra = tra[cols[2], :]
            scores = dot(nat[rows, cols[0]], k_tra)
            d_probs = dot(nat[rows, cols[3]], v_tra)
            row_max = jnp.max(scores, axis=1, keepdims=True)
            raised = jnp.exp2((scores - row_max) * (scale * LOG2E))
            probs = raised * (1.0 / jnp.sum(raised, axis=1, keepdims=True))
            probs_low = probs.astype(jnp.bfloat16)
            inner = jnp.sum(probs * d_probs, axis=1, keepdims=True)
            d_scores = (probs * (d_probs - inner) * scale).astype(jnp.bfloat16)
            out_ref[mine, rows] = dot(v_tra, probs_low, CONTRACT_COLS)
            dq_ref[mine, rows] = dot(k_tra, d_scores, CONTRACT_COLS)
            dv_part = dot(tra[cols[3], rows], probs_low)
            dk_part = dot(tra[cols[0], rows], d_scores)
            if step == 0:
                dv_ref[mine, :] = dv_part
                dk_ref[mine, :] = dk_part
            else:
                dv_ref[mine, :] += dv_part
                dk_ref[mine, :] += dk_part


def lepe(values, grads, taps, length, vertical):
    half = values.shape[0]
    lane = lax.broadcasted_iota(jnp.int32, (half, length), 1)
    if vertical:
        second = lax.rem(lane, 2) == 1
        apart, low, high = 2, lane < 2, lane >= length - 2

        def swap(source):
            return jnp.where(second, pltpu.roll(source, 1, 1), pltpu.roll(source, length - 1, 1))

        def tap(long_off, short_off):
            return 3 * (long_off + 1) + short_off + 1

    else:
        span = length // 2
        second = lane >= span
        place = lax.rem(lane, span)
        apart, low, high = 1, place == 0, place == span - 1

        def swap(source):
            return jnp.concatenate([source[:, span:], source[:, :span]], axis=1)

        def tap(long_off, short_off):
            return 3 * (short_off + 1) + long_off + 1

    def moved(source, long_off):
        if long_off == 0:
            return source
        if long_off > 0:
            return jnp.where(high, 0.0, pltpu.roll(source, length - apart, 1))
        return jnp.where(low, 0.0, pltpu.roll(source, apart, 1))

    def weight(index):
        return taps[:, index : index + 1]

    values_swap, grads_swap = swap(values), swap(grads)
    out = jnp.zeros((half, length), jnp.float32)
    d_values = jnp.zeros((half, length), jnp.float32)
    sums = [None] * 9
    for off in (-1, 0, 1):
        near, far = moved(values, off), moved(values_swap, off)
        out = out + weight(tap(off, 0)) * near
        out = out + jnp.where(second, weight(tap(off, -1)), weight(tap(off, 1))) * far
        d_values = d_values + weight(tap(off, 0)) * moved(grads, -off)
        d_values = d_values + jnp.where(second, weight(tap(off, 1)), weight(tap(off, -1))) * moved(grads_swap, -off)
        sums[tap(off, 0)] = jnp.sum(grads * near, axis=1, keepdims=True)
        cross = grads * far
        sums[tap(off, 1)] = jnp.sum(jnp.where(second, 0.0, cross), axis=1, keepdims=True)
        sums[tap(off, -1)] = jnp.sum(jnp.where(second, cross, 0.0), axis=1, keepdims=True)
    spot = lax.broadcasted_iota(jnp.int32, (half, 128), 1)
    tap_sums = jnp.zeros((half, 128), jnp.float32)
    for index in range(9):
        tap_sums = jnp.where(spot == index, sums[index], tap_sums)
    return out, d_values, tap_sums


def window(tokens, grads, w_nat, w_tra, w_out, taps, scratch, vertical):
    nat, tra, out_s, dq_s, dk_s, dv_s = scratch
    length = tokens.shape[0]
    half = w_out.shape[0]
    unit, _ = normalise(tokens)
    normed = unit.astype(jnp.bfloat16)
    nat[:, : 3 * half] = dot(normed, w_nat).astype(jnp.bfloat16)
    nat[:, 3 * half :] = dot(grads, w_out, CONTRACT_COLS).astype(jnp.bfloat16)
    tra[: 3 * half, :] = dot(w_tra, normed, CONTRACT_COLS).astype(jnp.bfloat16)
    tra[3 * half :, :] = dot(w_out, grads, CONTRACT_COLS).astype(jnp.bfloat16)
    heads = NUM_HEADS // 2
    attention(nat, tra, (out_s, dq_s, dk_s, dv_s), length, heads, half // heads)
    values = tra[2 * half : 3 * half, :].astype(jnp.float32)
    lifted = tra[3 * half :, :].astype(jnp.float32)
    near_out, near_dv, tap_sums = lepe(values, lifted, taps, length, vertical)
    attn = (out_s[...] + near_out).astype(jnp.bfloat16)
    grad_tokens = jnp.concatenate(
        [
            dq_s[...].astype(jnp.bfloat16),
            dk_s[...].astype(jnp.bfloat16),
            (dv_s[...] + near_dv).astype(jnp.bfloat16),
        ],
        axis=0,
    )
    return grad_tokens, dot(grad_tokens, normed), dot(attn, grads), tap_sums


def windows_kernel(vertical, x_ref, g_ref, wn_ref, wt_ref, wo_ref, tap_ref, gt_ref, qkv_ref, proj_ref, tap_out, *scratch):
    if vertical:
        length = x_ref.shape[0] * x_ref.shape[3]
        tokens = x_ref[:, 0, 0].astype(jnp.float32).reshape(length, x_ref.shape[4])
        grads = g_ref[:, 0, 0].astype(jnp.float32).reshape(length, x_ref.shape[4]).astype(jnp.bfloat16)
    else:
        tokens = x_ref[...].astype(jnp.float32)
        grads = g_ref[...]
    grad_tokens, qkv_part, proj_part, tap_part = window(
        tokens, grads, wn_ref[...], wt_ref[...], wo_ref[...], tap_ref[...], scratch, vertical
    )
    gt_ref[...] = grad_tokens.astype(jnp.float32).T.astype(jnp.bfloat16)

    @pl.when(pl.program_id(0) == 0)
    def _():
        qkv_ref[...] = qkv_part
        proj_ref[...] = proj_part
        tap_out[...] = tap_part

    @pl.when(pl.program_id(0) > 0)
    def _():
        qkv_ref[...] += qkv_part
        proj_ref[...] += proj_part
        tap_out[...] += tap_part


def run_windows(source_x, source_g, weights, vertical):
    w_nat, w_tra, w_out, taps = weights
    half = w_out.shape[0]
    channels = w_out.shape[1]
    if vertical:
        blocks, _, count, rows, _ = source_x.shape
        length = blocks * rows
        x_spec = pl.BlockSpec((blocks, 1, 1, rows, channels), lambda i: (0, 0, i, 0, 0))
        g_spec = pl.BlockSpec((blocks, 1, 1, rows, channels), lambda i: (0, 1, i, 0, 0))
    else:
        length = 1024
        count = source_x.shape[0] // length
        x_spec = pl.BlockSpec((length, channels), lambda i: (i, 0))
        g_spec = x_spec

    def whole(shape):
        return pl.BlockSpec(shape, lambda i: (0, 0))

    return pl.pallas_call(
        functools.partial(windows_kernel, vertical),
        grid=(count,),
        in_specs=[x_spec, g_spec] + [whole(w.shape) for w in weights],
        out_specs=[
            pl.BlockSpec((length, 3 * half), lambda i: (i, 0)),
            whole((3 * half, channels)),
            whole((half, channels)),
            whole((half, 128)),
        ],
        out_shape=[
            jax.ShapeDtypeStruct((count * length, 3 * half), jnp.bfloat16),
            jax.ShapeDtypeStruct((3 * half, channels), jnp.float32),
            jax.ShapeDtypeStruct((half, channels), jnp.float32),
            jax.ShapeDtypeStruct((half, 128), jnp.float32),
        ],
        scratch_shapes=[
            pltpu.VMEM((length, 4 * half), jnp.bfloat16),
            pltpu.VMEM((4 * half, length), jnp.bfloat16),
        ]
        + [pltpu.VMEM((half, length), jnp.float32)] * 4,
        compiler_params=pltpu.CompilerParams(vmem_limit_bytes=58 << 20),
        cost_estimate=pl.CostEstimate(flops=count * 3 * 10**9, bytes_accessed=4 << 20, transcendentals=count * 2 << 20),
    )(source_x, source_g, *weights)


def final_kernel(x_ref, g_ref, gh_ref, gv_ref, wh_ref, wv_ref, out_ref):
    unit, inv_std = normalise(x_ref[...].astype(jnp.float32))
    grad_unit = dot(gh_ref[...], wh_ref[...]) + dot(gv_ref[...], wv_ref[...])
    mean = jnp.mean(grad_unit, axis=1, keepdims=True)
    along = jnp.mean(grad_unit * unit, axis=1, keepdims=True)
    grad_norm = (grad_unit - mean - unit * along) * inv_std
    out_ref[...] = (g_ref[...].astype(jnp.float32) + grad_norm).astype(jnp.bfloat16)


def finish(tokens, grads, gt_h, gt_v, wt_h, wt_v):
    count, channels = tokens.shape
    block = min(count, 1024)
    row = pl.BlockSpec((block, channels), lambda i: (i, 0))
    wide = pl.BlockSpec((block, gt_h.shape[1]), lambda i: (i, 0))
    whole = pl.BlockSpec(wt_h.shape, lambda i: (0, 0))
    return pl.pallas_call(
        final_kernel,
        grid=(count // block,),
        in_specs=[row, row, wide, wide, whole, whole],
        out_specs=row,
        out_shape=jax.ShapeDtypeStruct((count, channels), jnp.bfloat16),
    )(tokens, grads, gt_h, gt_v, wt_h, wt_v)


PLANE = 32
DEPTH = 8


def reduce_kernel(parts, out, plane_buf, depth_buf, send_a, recv_a, send_b, recv_b, send_c, recv_c):
    row = lax.axis_index("rows")
    batch = lax.axis_index("batch")
    core = row % 2
    z_high = (row // 2) % 4
    mine = (row // 8) * 2 + core
    level = z_high * 2 + batch

    def plane_peer(other):
        return ((other // 2) * 8 + z_high * 2 + other % 2, batch)

    def depth_peer(other):
        return ((row // 8) * 8 + (other // 2) * 2 + core, other % 2)

    barrier = pltpu.get_barrier_semaphore()

    @pl.loop(1, PLANE)
    def _(step):
        pl.semaphore_signal(barrier, inc=1, device_id=plane_peer((mine + step) % PLANE), device_id_type=MESH)

    @pl.loop(1, DEPTH)
    def _(step):
        pl.semaphore_signal(barrier, inc=1, device_id=depth_peer((level + step) % DEPTH), device_id_type=MESH)

    pl.semaphore_wait(barrier, PLANE - 1 + DEPTH - 1)

    def copy_a(other, slot):
        return pltpu.make_async_remote_copy(
            src_ref=parts.at[other], dst_ref=plane_buf.at[slot], send_sem=send_a.at[other], recv_sem=recv_a.at[slot],
            device_id=plane_peer(other), device_id_type=MESH,
        )

    def copy_b(other, slot):
        return pltpu.make_async_remote_copy(
            src_ref=depth_buf.at[level], dst_ref=depth_buf.at[slot], send_sem=send_b.at[other], recv_sem=recv_b.at[slot],
            device_id=depth_peer(other), device_id_type=MESH,
        )

    def copy_c(other, slot):
        return pltpu.make_async_remote_copy(
            src_ref=out.at[mine], dst_ref=out.at[slot], send_sem=send_c.at[other], recv_sem=recv_c.at[slot],
            device_id=plane_peer(other), device_id_type=MESH,
        )

    @pl.loop(1, PLANE)
    def _(step):
        copy_a((mine + step) % PLANE, mine).start()

    plane_buf[mine] = parts[mine]

    @pl.loop(1, PLANE)
    def _(step):
        other = (mine + step) % PLANE
        copy_a(other, other).wait_recv()

    total = plane_buf[0]
    for index in range(1, PLANE):
        total = total + plane_buf[index]
    depth_buf[level] = total

    @pl.loop(1, DEPTH)
    def _(step):
        copy_b((level + step) % DEPTH, level).start()

    @pl.loop(1, DEPTH)
    def _(step):
        other = (level + step) % DEPTH
        copy_b(other, other).wait_recv()

    total = depth_buf[0]
    for index in range(1, DEPTH):
        total = total + depth_buf[index]
    out[mine] = total

    @pl.loop(1, PLANE)
    def _(step):
        copy_c((mine + step) % PLANE, mine).start()

    @pl.loop(1, PLANE)
    def _(step):
        other = (mine + step) % PLANE
        copy_c(other, other).wait_recv()

    @pl.loop(1, PLANE)
    def _(step):
        other = (mine + step) % PLANE
        copy_a(other, mine).wait_send()
        copy_c(other, mine).wait_send()

    @pl.loop(1, DEPTH)
    def _(step):
        copy_b((level + step) % DEPTH, level).wait_send()


def all_sum(parts):
    chunk = parts.shape[1:]
    vmem = pl.BlockSpec(memory_space=pltpu.VMEM)
    return pl.pallas_call(
        reduce_kernel,
        in_specs=[vmem],
        out_specs=vmem,
        out_shape=jax.ShapeDtypeStruct(parts.shape, jnp.float32),
        scratch_shapes=[
            pltpu.VMEM((PLANE,) + chunk, jnp.float32),
            pltpu.VMEM((DEPTH,) + chunk, jnp.float32),
            pltpu.SemaphoreType.DMA((PLANE,)),
            pltpu.SemaphoreType.DMA((PLANE,)),
            pltpu.SemaphoreType.DMA((DEPTH,)),
            pltpu.SemaphoreType.DMA((DEPTH,)),
            pltpu.SemaphoreType.DMA((PLANE,)),
            pltpu.SemaphoreType.DMA((PLANE,)),
        ],
        compiler_params=pltpu.CompilerParams(collective_id=0, has_side_effects=True),
    )(parts)


def body(features, grad_out, qkv_weight, proj_weight, lepe_weight):
    _, band_rows, map_cols, channels = features.shape
    half = channels // 2
    owners = lax.axis_size("rows")
    stripes = map_cols // owners // STRIPE
    tokens = features.reshape(-1, channels)
    grads = grad_out.reshape(-1, channels)

    def direction(first):
        w_nat = jnp.concatenate([qkv_weight[:, c + first : c + first + half] for c in (0, channels, 2 * channels)], axis=1)
        taps = lepe_weight[:, first : first + half].astype(jnp.float32).T
        return w_nat, w_nat.T, proj_weight[first : first + half], taps

    horiz, vert = direction(0), direction(half)

    def pack(source):
        split = source.reshape(band_rows, owners, stripes, STRIPE, channels).transpose(1, 2, 0, 3, 4)
        return split.reshape(owners, 1, stripes, band_rows * STRIPE, channels)

    sent = jnp.concatenate([pack(features), pack(grad_out)], axis=1)
    arrived = lax.all_to_all(sent, "rows", split_axis=0, concat_axis=0, tiled=True)
    gt_h, qkv_h, proj_h, tap_h = run_windows(tokens, grads, horiz, False)
    gt_v, qkv_v, proj_v, tap_v = run_windows(arrived, arrived, vert, True)
    back = gt_v.reshape(stripes, owners, band_rows * STRIPE, 3 * half).transpose(1, 0, 2, 3)
    returned = lax.all_to_all(back, "rows", split_axis=0, concat_axis=0, tiled=True)
    returned = returned.reshape(owners, stripes, band_rows, STRIPE, 3 * half).transpose(2, 0, 1, 3, 4)
    grad_features = finish(tokens, grads, gt_h, returned.reshape(-1, 3 * half), horiz[1], vert[1])

    tap_rows = jnp.concatenate([tap_h[:, :9], tap_v[:, :9]], axis=0).T
    main = jnp.concatenate([qkv_h, qkv_v, proj_h, proj_v], axis=0).reshape(PLANE, -1, channels)
    extra = jnp.pad(tap_rows, ((0, PLANE - 9), (0, 0))).reshape(PLANE, 1, channels)
    summed = all_sum(jnp.concatenate([main, extra], axis=1))
    total_tokens = lax.axis_size("batch") * owners * band_rows * map_cols
    summed = summed * total_tokens ** (-0.5)
    flat = summed[:, :-1].reshape(-1, channels)
    h_rows, v_rows = flat[: 3 * half], flat[3 * half : 6 * half]
    grad_qkv = jnp.concatenate(
        [piece[part * half : (part + 1) * half] for part in range(3) for piece in (h_rows, v_rows)], axis=0
    ).T
    return (
        grad_features.reshape(features.shape),
        grad_qkv,
        flat[6 * half :],
        summed[:9, -1],
    )


def solution(mesh):
    in_specs = (P("batch", "rows", None, None), P("batch", "rows", None, None), P(), P(), P())
    out_specs = (P("batch", "rows", None, None), P(), P(), P())
    return jax.shard_map(body, mesh=mesh, in_specs=in_specs, out_specs=out_specs, check_vma=False)
```

```python
import jax
import jax.numpy as jnp
from jax import lax
from jax.experimental import pallas as pl
from jax.experimental.pallas import tpu as pltpu
from jax.sharding import PartitionSpec as P

NUM_HEADS = 4
STRIPE = 2
EPSILON = 1e-05
LOG2E = 1.4426950408889634
COLS = (((1,), (1,)), ((), ()))
ROWS = (((0,), (0,)), ((), ()))
MESH = pl.DeviceIdType.MESH
QUERY_BLOCK = 512
CH = 128
SIZE = 32
LEN = 1024
BAND = 4
WIDTH = 512
OWNERS = 128
PLANE = 32
DEPTH = 8
PIECE = 64
SCALE = SIZE ** (-0.5)


def dot(left, right, dims=(((1,), (0,)), ((), ()))):
    return lax.dot_general(left, right, dims, preferred_element_type=jnp.float32)


def normalise(tokens):
    centred = tokens - jnp.mean(tokens, axis=1, keepdims=True)
    inv_std = lax.rsqrt(jnp.mean(centred * centred, axis=1, keepdims=True) + EPSILON)
    return centred * inv_std, inv_std


def attention(nat, tra, out_s, dq_s, dk_s, dv_s):
    k_tra = tra[SIZE : 2 * SIZE, :]
    v_tra = tra[2 * SIZE : 3 * SIZE, :]
    for step in range(LEN // QUERY_BLOCK):
        rows = slice(step * QUERY_BLOCK, (step + 1) * QUERY_BLOCK)
        scores = dot(nat[rows, :SIZE], k_tra)
        d_probs = dot(nat[rows, 3 * SIZE :], v_tra)
        row_max = jnp.max(scores, axis=1, keepdims=True)
        raised = jnp.exp2((scores - row_max) * (SCALE * LOG2E))
        probs = raised * (1.0 / jnp.sum(raised, axis=1, keepdims=True))
        probs_low = probs.astype(jnp.bfloat16)
        inner = jnp.sum(probs * d_probs, axis=1, keepdims=True)
        d_scores = (probs * (d_probs - inner) * SCALE).astype(jnp.bfloat16)
        out_s[:, rows] = dot(v_tra, probs_low, COLS)
        dq_s[:, rows] = dot(k_tra, d_scores, COLS)
        dv_part = dot(tra[3 * SIZE :, rows], probs_low)
        dk_part = dot(tra[:SIZE, rows], d_scores)
        if step == 0:
            dv_s[...] = dv_part
            dk_s[...] = dk_part
        else:
            dv_s[...] += dv_part
            dk_s[...] += dk_part


def lepe(values, grads, taps, vertical):
    lane = lax.broadcasted_iota(jnp.int32, (SIZE, LEN), 1)
    if vertical:
        second = lane % 2 == 1
        apart, low, high = 2, lane < 2, lane >= LEN - 2

        def swap(source):
            return jnp.where(second, pltpu.roll(source, 1, 1), pltpu.roll(source, LEN - 1, 1))

        def tap(long_off, short_off):
            return 3 * (long_off + 1) + short_off + 1

    else:
        span = LEN // 2
        second = lane >= span
        place = lane % span
        apart, low, high = 1, place == 0, place == span - 1

        def swap(source):
            return jnp.concatenate([source[:, span:], source[:, :span]], axis=1)

        def tap(long_off, short_off):
            return 3 * (short_off + 1) + long_off + 1

    def moved(source, long_off):
        if long_off == 0:
            return source
        if long_off > 0:
            return jnp.where(high, 0.0, pltpu.roll(source, LEN - apart, 1))
        return jnp.where(low, 0.0, pltpu.roll(source, apart, 1))

    def weight(index):
        return taps[:, index : index + 1]

    values_swap, grads_swap = swap(values), swap(grads)
    out = jnp.zeros((SIZE, LEN), jnp.float32)
    d_values = jnp.zeros((SIZE, LEN), jnp.float32)
    sums = [None] * 9
    for off in (-1, 0, 1):
        near, far = moved(values, off), moved(values_swap, off)
        out = out + weight(tap(off, 0)) * near
        out = out + jnp.where(second, weight(tap(off, -1)), weight(tap(off, 1))) * far
        d_values = d_values + weight(tap(off, 0)) * moved(grads, -off)
        d_values = d_values + jnp.where(second, weight(tap(off, 1)), weight(tap(off, -1))) * moved(grads_swap, -off)
        sums[tap(off, 0)] = jnp.sum(grads * near, axis=1, keepdims=True)
        cross = grads * far
        sums[tap(off, 1)] = jnp.sum(jnp.where(second, 0.0, cross), axis=1, keepdims=True)
        sums[tap(off, -1)] = jnp.sum(jnp.where(second, cross, 0.0), axis=1, keepdims=True)
    spot = lax.broadcasted_iota(jnp.int32, (SIZE, CH), 1)
    tap_sums = jnp.zeros((SIZE, CH), jnp.float32)
    for index in range(9):
        tap_sums = jnp.where(spot == index, sums[index], tap_sums)
    return out, d_values, tap_sums


def kernel(
    x_ref, g_ref, qkv_ref, proj_ref, lepe_ref,
    gf_out, qkv_out, proj_out, lepe_out,
    w_tra, taps, sent, arrived, back, returned, pair, nat, tra, out_s, dq_s, dk_s, dv_s, unit_h, acc, tap_acc,
    parts, plane_buf, depth_buf, total,
    send_f, recv_f, send_r, recv_r, send_a, recv_a, send_b, recv_b, send_c, recv_c,
):
    row = lax.axis_index("rows")
    batch = lax.axis_index("batch")
    core = row % 2
    z_high = (row // 2) % 4
    mine = (row // 8) * 2 + core
    level = z_high * 2 + batch

    def plane_peer(other):
        return ((other // 2) * 8 + z_high * 2 + other % 2, batch)

    def depth_peer(other):
        return ((row // 8) * 8 + (other // 2) * 2 + core, other % 2)

    barrier = pltpu.get_barrier_semaphore()

    @pl.loop(1, OWNERS)
    def _(step):
        pl.semaphore_signal(barrier, inc=1, device_id=((row + step) % OWNERS, batch), device_id_type=MESH)

    @pl.loop(0, 4)
    def _(step):
        pl.semaphore_signal(barrier, inc=1, device_id=depth_peer(step * 2 + 1 - batch), device_id_type=MESH)

    out_row = lax.broadcasted_iota(jnp.int32, (256, 256), 0)
    in_row = lax.broadcasted_iota(jnp.int32, (256, 256), 1)
    source_row = ((out_row // 2) % 4) * PIECE + ((out_row // 8) % 16) * 4 + (out_row // 128) * 2 + out_row % 2
    permute = (in_row == source_row).astype(jnp.float32).astype(jnp.bfloat16)
    for q in range(WIDTH // PIECE):
        both = jnp.concatenate(
            [
                jnp.concatenate(
                    [ref[r * WIDTH + q * PIECE : r * WIDTH + (q + 1) * PIECE, :] for r in range(BAND)], axis=0
                )
                for ref in (x_ref, g_ref)
            ],
            axis=1,
        )
        packed = dot(permute, both).reshape(2, 16, 8, 2 * CH).astype(jnp.bfloat16)
        sent[0, q * 16 : (q + 1) * 16] = packed[0]
        sent[1, q * 16 : (q + 1) * 16] = packed[1]

    qkv_tra = qkv_ref[...].astype(jnp.float32).T
    for head in range(NUM_HEADS):
        rows = [qkv_tra[part * CH + head * SIZE : part * CH + (head + 1) * SIZE, :] for part in range(3)]
        rows.append(jnp.zeros((SIZE, CH), jnp.float32))
        w_tra[head, :, :CH] = jnp.concatenate(rows, axis=0).astype(jnp.bfloat16)
        w_tra[head, : 3 * SIZE, CH:] = jnp.zeros((3 * SIZE, CH), jnp.bfloat16)
        w_tra[head, 3 * SIZE :, CH:] = proj_ref[head * SIZE : (head + 1) * SIZE, :]
    taps[...] = jnp.concatenate([lepe_ref[...].astype(jnp.float32), jnp.zeros((7, CH), jnp.float32)], axis=0).T
    acc[...] = jnp.zeros_like(acc)
    tap_acc[...] = jnp.zeros_like(tap_acc)

    pl.semaphore_wait(barrier, OWNERS - 1 + 4)

    def forward(stripe, other, slot):
        return pltpu.make_async_remote_copy(
            src_ref=sent.at[stripe, other], dst_ref=arrived.at[stripe, slot],
            send_sem=send_f.at[stripe], recv_sem=recv_f.at[stripe],
            device_id=(other, batch), device_id_type=MESH,
        )

    def backward(stripe, head, other, slot):
        return pltpu.make_async_remote_copy(
            src_ref=back.at[stripe, head, other], dst_ref=returned.at[stripe, head, slot],
            send_sem=send_r.at[stripe, head], recv_sem=recv_r.at[stripe, head],
            device_id=(other, batch), device_id_type=MESH,
        )

    def all_forward(stripe):
        return pltpu.make_async_remote_copy(
            src_ref=sent.at[stripe, pl.ds(0, OWNERS - 1)], dst_ref=arrived.at[stripe, pl.ds(0, OWNERS - 1)],
            send_sem=send_f.at[stripe], recv_sem=recv_f.at[stripe],
            device_id=((row + 1) % OWNERS, batch), device_id_type=MESH,
        )

    def all_backward(stripe, head):
        return pltpu.make_async_remote_copy(
            src_ref=back.at[stripe, head, pl.ds(0, OWNERS - 1)], dst_ref=returned.at[stripe, head, pl.ds(0, OWNERS - 1)],
            send_sem=send_r.at[stripe, head], recv_sem=recv_r.at[stripe, head],
            device_id=((row + 1) % OWNERS, batch), device_id_type=MESH,
        )

    for stripe in range(2):

        @pl.loop(1, OWNERS)
        def _(step):
            forward(stripe, (row + step) % OWNERS, row).start()

    for stripe in range(2):
        arrived[stripe, row] = sent[stripe, row]

    def one_head(head, vertical):
        nat[...] = dot(pair[...], w_tra[head], COLS).astype(jnp.bfloat16)
        tra[...] = dot(w_tra[head], pair[...], COLS).astype(jnp.bfloat16)
        attention(nat, tra, out_s, dq_s, dk_s, dv_s)
        values = tra[2 * SIZE : 3 * SIZE, :].astype(jnp.float32)
        lifted = tra[3 * SIZE :, :].astype(jnp.float32)
        channels = slice(head * SIZE, (head + 1) * SIZE)
        near_out, near_dv, tap_sums = lepe(values, lifted, taps[channels, :], vertical)
        whole = jnp.concatenate(
            [
                dq_s[...].astype(jnp.bfloat16),
                dk_s[...].astype(jnp.bfloat16),
                (dv_s[...] + near_dv).astype(jnp.bfloat16),
                (out_s[...] + near_out).astype(jnp.bfloat16),
            ],
            axis=0,
        )
        tap_acc[channels, :] += tap_sums
        part = dot(whole, pair[...])
        acc[head, : 3 * SIZE, :] += part[: 3 * SIZE, :CH]
        acc[head, 3 * SIZE :, :] += part[3 * SIZE :, CH:]
        return whole

    @pl.loop(0, 2)
    def _(turn):
        base = pl.multiple_of(turn * LEN, LEN)
        unit, _ = normalise(x_ref[pl.ds(base, LEN), :].astype(jnp.float32))
        pair[:, :CH] = unit.astype(jnp.bfloat16)
        pair[:, CH:] = g_ref[pl.ds(base, LEN), :]
        for head in range(2):
            whole = one_head(head, False)
            share = dot(whole, w_tra[head, :, :CH], ROWS)
            if head == 0:
                unit_h[pl.ds(base, LEN), :] = share
            else:
                unit_h[pl.ds(base, LEN), :] += share

        all_forward(turn).wait_recv()
        unit, _ = normalise(arrived[turn, :, :, :CH].astype(jnp.float32).reshape(LEN, CH))
        pair[:, :CH] = unit.astype(jnp.bfloat16)
        pair[:, CH:] = arrived[turn, :, :, CH:].astype(jnp.float32).reshape(LEN, CH).astype(jnp.bfloat16)
        for head in range(2):
            whole = one_head(2 + head, True)
            back[turn, head] = whole.astype(jnp.float32).T.reshape(OWNERS, 8, CH).astype(jnp.bfloat16)

            @pl.loop(1, OWNERS)
            def _(step):
                backward(turn, head, (row + step) % OWNERS, row).start()

            returned[turn, head, row] = back[turn, head, row]

    tap_rows = tap_acc[...].T
    for index in range(PLANE):
        head, place = index // 8, index % 8
        parts[index, :16, :] = acc[head, place * 16 : (place + 1) * 16, :]
        if index < 9:
            parts[index, 16:, :] = tap_rows[index : index + 1, :]
        else:
            parts[index, 16:, :] = jnp.zeros((1, CH), jnp.float32)

    def copy_a(other, slot):
        return pltpu.make_async_remote_copy(
            src_ref=parts.at[other], dst_ref=plane_buf.at[slot], send_sem=send_a.at[other], recv_sem=recv_a.at[slot],
            device_id=plane_peer(other), device_id_type=MESH,
        )

    def copy_b(other, slot):
        return pltpu.make_async_remote_copy(
            src_ref=depth_buf.at[level], dst_ref=depth_buf.at[slot], send_sem=send_b.at[other], recv_sem=recv_b.at[slot],
            device_id=depth_peer(other), device_id_type=MESH,
        )

    def copy_c(other, slot):
        return pltpu.make_async_remote_copy(
            src_ref=total.at[mine], dst_ref=total.at[slot], send_sem=send_c.at[other], recv_sem=recv_c.at[slot],
            device_id=plane_peer(other), device_id_type=MESH,
        )

    @pl.loop(1, PLANE)
    def _(step):
        copy_a((mine + step) % PLANE, mine).start()

    plane_buf[mine] = parts[mine]

    @pl.loop(1, PLANE)
    def _(step):
        other = (mine + step) % PLANE
        copy_a(other, other).wait_recv()

    sum_a = plane_buf[0]
    for index in range(1, PLANE):
        sum_a = sum_a + plane_buf[index]
    depth_buf[level] = sum_a

    @pl.loop(1, DEPTH)
    def _(step):
        copy_b((level + step) % DEPTH, level).start()

    @pl.loop(1, DEPTH)
    def _(step):
        other = (level + step) % DEPTH
        copy_b(other, other).wait_recv()

    sum_b = depth_buf[0]
    for index in range(1, DEPTH):
        sum_b = sum_b + depth_buf[index]
    total[mine] = sum_b

    @pl.loop(1, PLANE)
    def _(step):
        copy_c((mine + step) % PLANE, mine).start()

    for stripe in range(2):
        for head in range(2):
            all_backward(stripe, head).wait_recv()

    @pl.loop(0, WIDTH // PIECE)
    def _(q):
        owners = pl.ds(q * 16, 16)
        grads = jnp.concatenate(
            [
                jnp.concatenate(
                    [returned[j, head, owners].astype(jnp.float32).reshape(128, CH) for j in range(2)], axis=0
                ).astype(jnp.bfloat16)
                for head in range(2)
            ],
            axis=1,
        )
        ordered = dot(permute, grads, ROWS).astype(jnp.bfloat16)
        weights = jnp.concatenate([w_tra[2, :, :CH], w_tra[3, :, :CH]], axis=0)
        grad_v = dot(ordered, weights)
        for r in range(BAND):
            place = pl.ds(pl.multiple_of(r * WIDTH + q * PIECE, PIECE), PIECE)
            unit, inv_std = normalise(x_ref[place, :].astype(jnp.float32))
            grad_unit = unit_h[place, :] + grad_v[r * PIECE : (r + 1) * PIECE, :]
            mean = jnp.mean(grad_unit, axis=1, keepdims=True)
            along = jnp.mean(grad_unit * unit, axis=1, keepdims=True)
            grad_norm = (grad_unit - mean - unit * along) * inv_std
            gf_out[place, :] = (g_ref[place, :].astype(jnp.float32) + grad_norm).astype(jnp.bfloat16)

    @pl.loop(1, PLANE)
    def _(step):
        other = (mine + step) % PLANE
        copy_c(other, other).wait_recv()

    z = (2 * 512 * 512) ** (-0.5)

    def rows_of(head, start):
        return [total[head * 8 + (start + half * 16) // 16, :16, :] for half in range(2)]

    for part in range(3):
        pieces = [piece for head in range(NUM_HEADS) for piece in rows_of(head, part * SIZE)]
        qkv_out[:, part * CH : (part + 1) * CH] = jnp.concatenate(pieces, axis=0).T * z
    proj_out[...] = jnp.concatenate([piece for head in range(NUM_HEADS) for piece in rows_of(head, 3 * SIZE)], axis=0) * z
    lepe_out[...] = jnp.concatenate([total[index, 16:, :] for index in range(9)], axis=0) * z

    for stripe in range(2):
        all_forward(stripe).wait_send()
        for head in range(2):
            all_backward(stripe, head).wait_send()

    @pl.loop(1, PLANE)
    def _(step):
        other = (mine + step) % PLANE
        copy_a(other, mine).wait_send()
        copy_c(other, mine).wait_send()

    @pl.loop(1, DEPTH)
    def _(step):
        copy_b((level + step) % DEPTH, level).wait_send()


def body(features, grad_out, qkv_weight, proj_weight, lepe_weight):
    tokens = BAND * WIDTH
    vmem = pl.BlockSpec(memory_space=pltpu.VMEM)
    low, wide = jnp.bfloat16, jnp.float32
    dma = pltpu.SemaphoreType.DMA
    grad_features, grad_qkv, grad_proj, grad_lepe = pl.pallas_call(
        kernel,
        in_specs=[vmem] * 5,
        out_specs=[vmem] * 4,
        out_shape=[
            jax.ShapeDtypeStruct((tokens, CH), low),
            jax.ShapeDtypeStruct((CH, 3 * CH), wide),
            jax.ShapeDtypeStruct((CH, CH), wide),
            jax.ShapeDtypeStruct((9, CH), wide),
        ],
        scratch_shapes=[
            pltpu.VMEM((NUM_HEADS, CH, 2 * CH), low),
            pltpu.VMEM((CH, 16), wide),
            pltpu.VMEM((2, OWNERS, 8, 2 * CH), low),
            pltpu.VMEM((2, OWNERS, 8, 2 * CH), low),
            pltpu.VMEM((2, 2, OWNERS, 8, CH), low),
            pltpu.VMEM((2, 2, OWNERS, 8, CH), low),
            pltpu.VMEM((LEN, 2 * CH), low),
            pltpu.VMEM((LEN, CH), low),
            pltpu.VMEM((CH, LEN), low),
            pltpu.VMEM((SIZE, LEN), wide),
            pltpu.VMEM((SIZE, LEN), wide),
            pltpu.VMEM((SIZE, LEN), wide),
            pltpu.VMEM((SIZE, LEN), wide),
            pltpu.VMEM((tokens, CH), wide),
            pltpu.VMEM((NUM_HEADS, CH, CH), wide),
            pltpu.VMEM((CH, CH), wide),
            pltpu.VMEM((PLANE, 17, CH), wide),
            pltpu.VMEM((PLANE, 17, CH), wide),
            pltpu.VMEM((DEPTH, 17, CH), wide),
            pltpu.VMEM((PLANE, 17, CH), wide),
            dma((2,)), dma((2,)), dma((2, 2)), dma((2, 2)),
            dma((PLANE,)), dma((PLANE,)), dma((DEPTH,)), dma((DEPTH,)), dma((PLANE,)), dma((PLANE,)),
        ],
        compiler_params=pltpu.CompilerParams(
            collective_id=0, has_side_effects=True, vmem_limit_bytes=60 << 20
        ),
    )(features.reshape(tokens, CH), grad_out.reshape(tokens, CH), qkv_weight, proj_weight, lepe_weight)
    return grad_features.reshape(features.shape), grad_qkv, grad_proj, grad_lepe


def solution(mesh):
    in_specs = (P("batch", "rows", None, None), P("batch", "rows", None, None), P(), P(), P())
    out_specs = (P("batch", "rows", None, None), P(), P(), P())
    return jax.shard_map(body, mesh=mesh, in_specs=in_specs, out_specs=out_specs, check_vma=False)
```

```python
import jax
import jax.numpy as jnp
from jax import lax
from jax.experimental import pallas as pl
from jax.experimental.pallas import tpu as pltpu
from jax.sharding import PartitionSpec as P

NUM_HEADS = 4
STRIPE = 2
EPSILON = 1e-05
LOG2E = 1.4426950408889634
COLS = (((1,), (1,)), ((), ()))
ROWS = (((0,), (0,)), ((), ()))
MESH = pl.DeviceIdType.MESH
QUERY_BLOCK = 512
CH = 128
SIZE = 32
LEN = 1024
BAND = 4
WIDTH = 512
OWNERS = 128
PLANE = 32
DEPTH = 8
PIECE = 64
SCALE = SIZE ** (-0.5)


def dot(left, right, dims=(((1,), (0,)), ((), ()))):
    return lax.dot_general(left, right, dims, preferred_element_type=jnp.float32)


def normalise(tokens):
    centred = tokens - jnp.mean(tokens, axis=1, keepdims=True)
    inv_std = lax.rsqrt(jnp.mean(centred * centred, axis=1, keepdims=True) + EPSILON)
    return centred * inv_std, inv_std


def attention(nat, tra, out_s, dq_s, dk_s, dv_s):
    k_tra = tra[SIZE : 2 * SIZE, :]
    v_tra = tra[2 * SIZE : 3 * SIZE, :]
    for step in range(LEN // QUERY_BLOCK):
        rows = slice(step * QUERY_BLOCK, (step + 1) * QUERY_BLOCK)
        scores = dot(nat[rows, :SIZE], k_tra)
        d_probs = dot(nat[rows, 3 * SIZE :], v_tra)
        row_max = jnp.max(scores, axis=1, keepdims=True)
        raised = jnp.exp2((scores - row_max) * (SCALE * LOG2E))
        probs = raised * (1.0 / jnp.sum(raised, axis=1, keepdims=True))
        probs_low = probs.astype(jnp.bfloat16)
        inner = jnp.sum(probs * d_probs, axis=1, keepdims=True)
        d_scores = (probs * (d_probs - inner) * SCALE).astype(jnp.bfloat16)
        out_s[:, rows] = dot(v_tra, probs_low, COLS)
        dq_s[:, rows] = dot(k_tra, d_scores, COLS)
        dv_part = dot(tra[3 * SIZE :, rows], probs_low)
        dk_part = dot(tra[:SIZE, rows], d_scores)
        if step == 0:
            dv_s[...] = dv_part
            dk_s[...] = dk_part
        else:
            dv_s[...] += dv_part
            dk_s[...] += dk_part


def lepe(values, grads, taps, vertical):
    lane = lax.broadcasted_iota(jnp.int32, (SIZE, LEN), 1)
    if vertical:
        second = lane % 2 == 1
        apart, low, high = 2, lane < 2, lane >= LEN - 2

        def swap(source):
            return jnp.where(second, pltpu.roll(source, 1, 1), pltpu.roll(source, LEN - 1, 1))

        def tap(long_off, short_off):
            return 3 * (long_off + 1) + short_off + 1

    else:
        span = LEN // 2
        second = lane >= span
        place = lane % span
        apart, low, high = 1, place == 0, place == span - 1

        def swap(source):
            return jnp.concatenate([source[:, span:], source[:, :span]], axis=1)

        def tap(long_off, short_off):
            return 3 * (short_off + 1) + long_off + 1

    def moved(source, long_off):
        if long_off == 0:
            return source
        if long_off > 0:
            return jnp.where(high, 0.0, pltpu.roll(source, LEN - apart, 1))
        return jnp.where(low, 0.0, pltpu.roll(source, apart, 1))

    def weight(index):
        return taps[:, index : index + 1]

    values_swap, grads_swap = swap(values), swap(grads)
    out = jnp.zeros((SIZE, LEN), jnp.float32)
    d_values = jnp.zeros((SIZE, LEN), jnp.float32)
    sums = [None] * 9
    for off in (-1, 0, 1):
        near, far = moved(values, off), moved(values_swap, off)
        out = out + weight(tap(off, 0)) * near
        out = out + jnp.where(second, weight(tap(off, -1)), weight(tap(off, 1))) * far
        d_values = d_values + weight(tap(off, 0)) * moved(grads, -off)
        d_values = d_values + jnp.where(second, weight(tap(off, 1)), weight(tap(off, -1))) * moved(grads_swap, -off)
        sums[tap(off, 0)] = jnp.sum(grads * near, axis=1, keepdims=True)
        cross = grads * far
        sums[tap(off, 1)] = jnp.sum(jnp.where(second, 0.0, cross), axis=1, keepdims=True)
        sums[tap(off, -1)] = jnp.sum(jnp.where(second, cross, 0.0), axis=1, keepdims=True)
    spot = lax.broadcasted_iota(jnp.int32, (SIZE, CH), 1)
    tap_sums = jnp.zeros((SIZE, CH), jnp.float32)
    for index in range(9):
        tap_sums = jnp.where(spot == index, sums[index], tap_sums)
    return out, d_values, tap_sums


def kernel(
    x_ref, g_ref, qkv_ref, proj_ref, lepe_ref,
    gf_out, qkv_out, proj_out, lepe_out,
    w_tra, taps, sent, arrived, back, returned, pair, nat, tra, out_s, dq_s, dk_s, dv_s, unit_h, acc, tap_acc,
    parts_h, plane_h, depth_h, total_h, parts_v, plane_v, depth_v, total_v, unit_s, inv_s,
    send_f, recv_f, send_r, recv_r, send_a, recv_a, send_b, recv_b, send_c, recv_c,
):
    row = lax.axis_index("rows")
    batch = lax.axis_index("batch")
    core = row % 2
    z_high = (row // 2) % 4
    mine = (row // 8) * 2 + core
    level = z_high * 2 + batch

    def plane_peer(other):
        return ((other // 2) * 8 + z_high * 2 + other % 2, batch)

    def depth_peer(other):
        return ((row // 8) * 8 + (other // 2) * 2 + core, other % 2)

    barrier = pltpu.get_barrier_semaphore()

    @pl.loop(1, OWNERS)
    def _(step):
        pl.semaphore_signal(barrier, inc=1, device_id=((row + step) % OWNERS, batch), device_id_type=MESH)

    @pl.loop(0, 4)
    def _(step):
        pl.semaphore_signal(barrier, inc=1, device_id=depth_peer(step * 2 + 1 - batch), device_id_type=MESH)

    out_row = lax.broadcasted_iota(jnp.int32, (256, 256), 0)
    in_row = lax.broadcasted_iota(jnp.int32, (256, 256), 1)
    source_row = ((out_row // 2) % 4) * PIECE + ((out_row // 8) % 16) * 4 + (out_row // 128) * 2 + out_row % 2
    permute = (in_row == source_row).astype(jnp.float32).astype(jnp.bfloat16)
    for q in range(WIDTH // PIECE):
        both = jnp.concatenate(
            [
                jnp.concatenate(
                    [ref[r * WIDTH + q * PIECE : r * WIDTH + (q + 1) * PIECE, :] for r in range(BAND)], axis=0
                )
                for ref in (x_ref, g_ref)
            ],
            axis=1,
        )
        packed = dot(permute, both).reshape(2, 16, 8, 2 * CH).astype(jnp.bfloat16)
        sent[0, q * 16 : (q + 1) * 16] = packed[0]
        sent[1, q * 16 : (q + 1) * 16] = packed[1]

    qkv_tra = qkv_ref[...].astype(jnp.float32).T
    for head in range(NUM_HEADS):
        rows = [qkv_tra[part * CH + head * SIZE : part * CH + (head + 1) * SIZE, :] for part in range(3)]
        rows.append(jnp.zeros((SIZE, CH), jnp.float32))
        w_tra[head, :, :CH] = jnp.concatenate(rows, axis=0).astype(jnp.bfloat16)
        w_tra[head, : 3 * SIZE, CH:] = jnp.zeros((3 * SIZE, CH), jnp.bfloat16)
        w_tra[head, 3 * SIZE :, CH:] = proj_ref[head * SIZE : (head + 1) * SIZE, :]
    taps[...] = jnp.concatenate([lepe_ref[...].astype(jnp.float32), jnp.zeros((7, CH), jnp.float32)], axis=0).T
    acc[...] = jnp.zeros_like(acc)
    tap_acc[...] = jnp.zeros_like(tap_acc)

    pl.semaphore_wait(barrier, OWNERS - 1 + 4)

    def forward(stripe, other, slot):
        return pltpu.make_async_remote_copy(
            src_ref=sent.at[stripe, other], dst_ref=arrived.at[stripe, slot],
            send_sem=send_f.at[stripe], recv_sem=recv_f.at[stripe],
            device_id=(other, batch), device_id_type=MESH,
        )

    def backward(stripe, head, other, slot):
        return pltpu.make_async_remote_copy(
            src_ref=back.at[stripe, head, other], dst_ref=returned.at[stripe, head, slot],
            send_sem=send_r.at[stripe, head], recv_sem=recv_r.at[stripe, head],
            device_id=(other, batch), device_id_type=MESH,
        )

    def all_forward(stripe):
        return pltpu.make_async_remote_copy(
            src_ref=sent.at[stripe, pl.ds(0, OWNERS - 1)], dst_ref=arrived.at[stripe, pl.ds(0, OWNERS - 1)],
            send_sem=send_f.at[stripe], recv_sem=recv_f.at[stripe],
            device_id=((row + 1) % OWNERS, batch), device_id_type=MESH,
        )

    def all_backward(stripe, head):
        return pltpu.make_async_remote_copy(
            src_ref=back.at[stripe, head, pl.ds(0, OWNERS - 1)], dst_ref=returned.at[stripe, head, pl.ds(0, OWNERS - 1)],
            send_sem=send_r.at[stripe, head], recv_sem=recv_r.at[stripe, head],
            device_id=((row + 1) % OWNERS, batch), device_id_type=MESH,
        )

    bufs = ((parts_h, plane_h, depth_h, total_h), (parts_v, plane_v, depth_v, total_v))

    def copy_a(side, other, slot):
        return pltpu.make_async_remote_copy(
            src_ref=bufs[side][0].at[other], dst_ref=bufs[side][1].at[slot],
            send_sem=send_a.at[side, other], recv_sem=recv_a.at[side, slot],
            device_id=plane_peer(other), device_id_type=MESH,
        )

    def copy_b(side, other, slot):
        return pltpu.make_async_remote_copy(
            src_ref=bufs[side][2].at[level], dst_ref=bufs[side][2].at[slot],
            send_sem=send_b.at[side, other], recv_sem=recv_b.at[side, slot],
            device_id=depth_peer(other), device_id_type=MESH,
        )

    def copy_c(side, other, slot):
        return pltpu.make_async_remote_copy(
            src_ref=bufs[side][3].at[mine], dst_ref=bufs[side][3].at[slot],
            send_sem=send_c.at[side, other], recv_sem=recv_c.at[side, slot],
            device_id=plane_peer(other), device_id_type=MESH,
        )

    def start_a(side):
        parts, plane = bufs[side][:2]
        for index in range(PLANE):
            head, place = 2 * side + index // 16, index % 16
            parts[index, :8, :] = acc[head, place * 8 : (place + 1) * 8, :]
        if side == 1:
            tap_rows = tap_acc[...].T
            for index in range(9):
                parts[index, 8:, :] = tap_rows[index : index + 1, :]
            for index in range(9, PLANE):
                parts[index, 8:, :] = jnp.zeros((1, CH), jnp.float32)

        @pl.loop(1, PLANE)
        def _(step):
            copy_a(side, (mine + step) % PLANE, mine).start()

        plane[mine] = parts[mine]

    def start_b(side):
        _, plane, depth, _ = bufs[side]

        @pl.loop(1, PLANE)
        def _(step):
            other = (mine + step) % PLANE
            copy_a(side, other, other).wait_recv()

        sums = [plane[index] for index in range(PLANE)]
        while len(sums) > 1:
            sums = [one + two for one, two in zip(sums[::2], sums[1::2])]
        depth[level] = sums[0]

        @pl.loop(1, DEPTH)
        def _(step):
            copy_b(side, (level + step) % DEPTH, level).start()

    def start_c(side):
        _, _, depth, total = bufs[side]

        @pl.loop(1, DEPTH)
        def _(step):
            other = (level + step) % DEPTH
            copy_b(side, other, other).wait_recv()

        sums = [depth[index] for index in range(DEPTH)]
        while len(sums) > 1:
            sums = [one + two for one, two in zip(sums[::2], sums[1::2])]
        total[mine] = sums[0]

        @pl.loop(1, PLANE)
        def _(step):
            copy_c(side, (mine + step) % PLANE, mine).start()

    for stripe in range(2):

        @pl.loop(1, OWNERS)
        def _(step):
            forward(stripe, (row + step) % OWNERS, row).start()

    for stripe in range(2):
        arrived[stripe, row] = sent[stripe, row]

    def one_head(head, vertical):
        nat[...] = dot(pair[...], w_tra[head], COLS).astype(jnp.bfloat16)
        tra[...] = dot(w_tra[head], pair[...], COLS).astype(jnp.bfloat16)
        attention(nat, tra, out_s, dq_s, dk_s, dv_s)
        values = tra[2 * SIZE : 3 * SIZE, :].astype(jnp.float32)
        lifted = tra[3 * SIZE :, :].astype(jnp.float32)
        channels = slice(head * SIZE, (head + 1) * SIZE)
        near_out, near_dv, tap_sums = lepe(values, lifted, taps[channels, :], vertical)
        whole = jnp.concatenate(
            [
                dq_s[...].astype(jnp.bfloat16),
                dk_s[...].astype(jnp.bfloat16),
                (dv_s[...] + near_dv).astype(jnp.bfloat16),
                (out_s[...] + near_out).astype(jnp.bfloat16),
            ],
            axis=0,
        )
        tap_acc[channels, :] += tap_sums
        part = dot(whole, pair[...])
        acc[head, : 3 * SIZE, :] += part[: 3 * SIZE, :CH]
        acc[head, 3 * SIZE :, :] += part[3 * SIZE :, CH:]
        return whole

    @pl.loop(0, 2)
    def _(turn):
        base = pl.multiple_of(turn * LEN, LEN)
        unit, _ = normalise(x_ref[pl.ds(base, LEN), :].astype(jnp.float32))
        pair[:, :CH] = unit.astype(jnp.bfloat16)
        pair[:, CH:] = g_ref[pl.ds(base, LEN), :]
        for head in range(2):
            whole = one_head(head, False)
            share = dot(whole, w_tra[head, :, :CH], ROWS)
            if head == 0:
                unit_h[pl.ds(base, LEN), :] = share
            else:
                unit_h[pl.ds(base, LEN), :] += share

    start_a(0)

    @pl.loop(0, 2)
    def _(turn):
        all_forward(turn).wait_recv()
        unit, _ = normalise(arrived[turn, :, :, :CH].astype(jnp.float32).reshape(LEN, CH))
        pair[:, :CH] = unit.astype(jnp.bfloat16)
        pair[:, CH:] = arrived[turn, :, :, CH:].astype(jnp.float32).reshape(LEN, CH).astype(jnp.bfloat16)
        for head in range(2):
            whole = one_head(2 + head, True)
            if head == 1:

                @pl.when(turn == 1)
                def _():
                    start_a(1)

            back[turn, head] = whole.astype(jnp.float32).T.reshape(OWNERS, 8, CH).astype(jnp.bfloat16)

            @pl.loop(1, OWNERS)
            def _(step):
                backward(turn, head, (row + step) % OWNERS, row).start()

            returned[turn, head, row] = back[turn, head, row]

        @pl.when(turn == 0)
        def _():
            start_b(0)

    start_c(0)
    for index in range((BAND * WIDTH) // 256):
        place = slice(index * 256, (index + 1) * 256)
        unit, inv_std = normalise(x_ref[place, :].astype(jnp.float32))
        unit_s[place, :] = unit
        inv_s[place, :] = jnp.broadcast_to(inv_std, (256, CH))
    start_b(1)
    start_c(1)

    for stripe in range(2):
        for head in range(2):
            all_backward(stripe, head).wait_recv()

    @pl.loop(0, WIDTH // PIECE)
    def _(q):
        owners = pl.ds(q * 16, 16)
        grads = jnp.concatenate(
            [
                jnp.concatenate(
                    [returned[j, head, owners].astype(jnp.float32).reshape(128, CH) for j in range(2)], axis=0
                ).astype(jnp.bfloat16)
                for head in range(2)
            ],
            axis=1,
        )
        ordered = dot(permute, grads, ROWS).astype(jnp.bfloat16)
        weights = jnp.concatenate([w_tra[2, :, :CH], w_tra[3, :, :CH]], axis=0)
        grad_v = dot(ordered, weights)
        for r in range(BAND):
            place = pl.ds(pl.multiple_of(r * WIDTH + q * PIECE, PIECE), PIECE)
            unit, inv_std = unit_s[place, :], inv_s[place, :]
            grad_unit = unit_h[place, :] + grad_v[r * PIECE : (r + 1) * PIECE, :]
            mean = jnp.mean(grad_unit, axis=1, keepdims=True)
            along = jnp.mean(grad_unit * unit, axis=1, keepdims=True)
            grad_norm = (grad_unit - mean - unit * along) * inv_std
            gf_out[place, :] = (g_ref[place, :].astype(jnp.float32) + grad_norm).astype(jnp.bfloat16)

    for side in range(2):

        @pl.loop(1, PLANE)
        def _(step):
            other = (mine + step) % PLANE
            copy_c(side, other, other).wait_recv()

    z = (2 * 512 * 512) ** (-0.5)

    def rows_of(head, start):
        total = bufs[head // 2][3]
        return [total[(head % 2) * 16 + start // 8 + part, :8, :] for part in range(SIZE // 8)]

    for part in range(3):
        pieces = [piece for head in range(NUM_HEADS) for piece in rows_of(head, part * SIZE)]
        qkv_out[:, part * CH : (part + 1) * CH] = jnp.concatenate(pieces, axis=0).T * z
    proj_out[...] = jnp.concatenate([piece for head in range(NUM_HEADS) for piece in rows_of(head, 3 * SIZE)], axis=0) * z
    lepe_out[...] = jnp.concatenate([total_v[index, 8:, :] for index in range(9)], axis=0) * z

    for stripe in range(2):
        all_forward(stripe).wait_send()
        for head in range(2):
            all_backward(stripe, head).wait_send()

    for side in range(2):

        @pl.loop(1, PLANE)
        def _(step):
            other = (mine + step) % PLANE
            copy_a(side, other, mine).wait_send()
            copy_c(side, other, mine).wait_send()

        @pl.loop(1, DEPTH)
        def _(step):
            copy_b(side, (level + step) % DEPTH, level).wait_send()


def hand_over(*refs):
    for source, target in zip(refs[:4], refs[4:]):
        target[...] = source[...]


def body(features, grad_out, qkv_weight, proj_weight, lepe_weight):
    tokens = BAND * WIDTH
    vmem = pl.BlockSpec(memory_space=pltpu.VMEM)
    low, wide = jnp.bfloat16, jnp.float32
    dma = pltpu.SemaphoreType.DMA
    grad_features, grad_qkv, grad_proj, grad_lepe = pl.pallas_call(
        kernel,
        in_specs=[vmem] * 5,
        out_specs=[vmem] * 4,
        out_shape=[
            jax.ShapeDtypeStruct((tokens, CH), low),
            jax.ShapeDtypeStruct((CH, 3 * CH), wide),
            jax.ShapeDtypeStruct((CH, CH), wide),
            jax.ShapeDtypeStruct((9, CH), wide),
        ],
        scratch_shapes=[
            pltpu.VMEM((NUM_HEADS, CH, 2 * CH), low),
            pltpu.VMEM((CH, 16), wide),
            pltpu.VMEM((2, OWNERS, 8, 2 * CH), low),
            pltpu.VMEM((2, OWNERS, 8, 2 * CH), low),
            pltpu.VMEM((2, 2, OWNERS, 8, CH), low),
            pltpu.VMEM((2, 2, OWNERS, 8, CH), low),
            pltpu.VMEM((LEN, 2 * CH), low),
            pltpu.VMEM((LEN, CH), low),
            pltpu.VMEM((CH, LEN), low),
            pltpu.VMEM((SIZE, LEN), wide),
            pltpu.VMEM((SIZE, LEN), wide),
            pltpu.VMEM((SIZE, LEN), wide),
            pltpu.VMEM((SIZE, LEN), wide),
            pltpu.VMEM((tokens, CH), wide),
            pltpu.VMEM((NUM_HEADS, CH, CH), wide),
            pltpu.VMEM((CH, CH), wide),
            pltpu.VMEM((PLANE, 8, CH), wide),
            pltpu.VMEM((PLANE, 8, CH), wide),
            pltpu.VMEM((DEPTH, 8, CH), wide),
            pltpu.VMEM((PLANE, 8, CH), wide),
            pltpu.VMEM((PLANE, 9, CH), wide),
            pltpu.VMEM((PLANE, 9, CH), wide),
            pltpu.VMEM((DEPTH, 9, CH), wide),
            pltpu.VMEM((PLANE, 9, CH), wide),
            pltpu.VMEM((tokens, CH), wide),
            pltpu.VMEM((tokens, CH), wide),
            dma((2,)), dma((2,)), dma((2, 2)), dma((2, 2)),
            dma((2, PLANE)), dma((2, PLANE)), dma((2, DEPTH)), dma((2, DEPTH)), dma((2, PLANE)), dma((2, PLANE)),
        ],
        compiler_params=pltpu.CompilerParams(
            collective_id=0, has_side_effects=True, vmem_limit_bytes=60 << 20
        ),
    )(features.reshape(tokens, CH), grad_out.reshape(tokens, CH), qkv_weight, proj_weight, lepe_weight)
    results = pl.pallas_call(
        hand_over,
        in_specs=[vmem] * 4,
        out_specs=[vmem] * 4,
        out_shape=[jax.ShapeDtypeStruct(a.shape, a.dtype) for a in (grad_features, grad_qkv, grad_proj, grad_lepe)],
    )(grad_features, grad_qkv, grad_proj, grad_lepe)
    return (results[0].reshape(features.shape), *results[1:])


def solution(mesh):
    in_specs = (P("batch", "rows", None, None), P("batch", "rows", None, None), P(), P(), P())
    out_specs = (P("batch", "rows", None, None), P(), P(), P())
    return jax.shard_map(body, mesh=mesh, in_specs=in_specs, out_specs=out_specs, check_vma=False)
```

```python
import jax
import jax.numpy as jnp
from jax import lax
from jax.experimental import pallas as pl
from jax.experimental.pallas import tpu as pltpu
from jax.sharding import PartitionSpec as P

NUM_HEADS = 4
STRIPE = 2
EPSILON = 1e-05
LOG2E = 1.4426950408889634
COLS = (((1,), (1,)), ((), ()))
ROWS = (((0,), (0,)), ((), ()))
MESH = pl.DeviceIdType.MESH
QUERY_BLOCK = 1024
CH = 128
SIZE = 32
LEN = 1024
BAND = 4
WIDTH = 512
OWNERS = 128
PLANE = 32
DEPTH = 8
PIECE = 64
SCALE = SIZE ** (-0.5)


def dot(left, right, dims=(((1,), (0,)), ((), ()))):
    return lax.dot_general(left, right, dims, preferred_element_type=jnp.float32)


def normalise(tokens):
    centred = tokens - jnp.mean(tokens, axis=1, keepdims=True)
    inv_std = lax.rsqrt(jnp.mean(centred * centred, axis=1, keepdims=True) + EPSILON)
    return centred * inv_std, inv_std


def attention(nat, tra, out_s, dq_s, dk_s, dv_s):
    k_tra = tra[SIZE : 2 * SIZE, :]
    v_tra = tra[2 * SIZE : 3 * SIZE, :]
    for step in range(LEN // QUERY_BLOCK):
        rows = slice(step * QUERY_BLOCK, (step + 1) * QUERY_BLOCK)
        scores = dot(nat[rows, :SIZE], k_tra)
        d_probs = dot(nat[rows, 3 * SIZE :], v_tra)
        row_max = jnp.max(scores, axis=1, keepdims=True)
        raised = jnp.exp2((scores - row_max) * (SCALE * LOG2E))
        probs = raised * (1.0 / jnp.sum(raised, axis=1, keepdims=True))
        probs_low = probs.astype(jnp.bfloat16)
        inner = jnp.sum(probs * d_probs, axis=1, keepdims=True)
        d_scores = (probs * (d_probs - inner) * SCALE).astype(jnp.bfloat16)
        out_s[:, rows] = dot(probs_low, nat[:, 2 * SIZE : 3 * SIZE]).T
        dq_s[:, rows] = dot(d_scores, nat[:, SIZE : 2 * SIZE]).T
        dv_part = dot(tra[3 * SIZE :, rows], probs_low)
        dk_part = dot(tra[:SIZE, rows], d_scores)
        if step == 0:
            dv_s[...] = dv_part
            dk_s[...] = dk_part
        else:
            dv_s[...] += dv_part
            dk_s[...] += dk_part


def lepe(values, grads, taps, vertical):
    lane = lax.broadcasted_iota(jnp.int32, (SIZE, LEN), 1)
    if vertical:
        second = lane % 2 == 1
        apart, low, high = 2, lane < 2, lane >= LEN - 2

        def swap(source):
            return jnp.where(second, pltpu.roll(source, 1, 1), pltpu.roll(source, LEN - 1, 1))

        def tap(long_off, short_off):
            return 3 * (long_off + 1) + short_off + 1

    else:
        span = LEN // 2
        second = lane >= span
        place = lane % span
        apart, low, high = 1, place == 0, place == span - 1

        def swap(source):
            return jnp.concatenate([source[:, span:], source[:, :span]], axis=1)

        def tap(long_off, short_off):
            return 3 * (short_off + 1) + long_off + 1

    def moved(source, long_off):
        if long_off == 0:
            return source
        if long_off > 0:
            return jnp.where(high, 0.0, pltpu.roll(source, LEN - apart, 1))
        return jnp.where(low, 0.0, pltpu.roll(source, apart, 1))

    def weight(index):
        return taps[:, index : index + 1]

    values_swap, grads_swap = swap(values), swap(grads)
    out = jnp.zeros((SIZE, LEN), jnp.float32)
    d_values = jnp.zeros((SIZE, LEN), jnp.float32)
    sums = [None] * 9
    for off in (-1, 0, 1):
        near, far = moved(values, off), moved(values_swap, off)
        out = out + weight(tap(off, 0)) * near
        out = out + jnp.where(second, weight(tap(off, -1)), weight(tap(off, 1))) * far
        d_values = d_values + weight(tap(off, 0)) * moved(grads, -off)
        d_values = d_values + jnp.where(second, weight(tap(off, 1)), weight(tap(off, -1))) * moved(grads_swap, -off)
        sums[tap(off, 0)] = jnp.sum(grads * near, axis=1, keepdims=True)
        cross = grads * far
        sums[tap(off, 1)] = jnp.sum(jnp.where(second, 0.0, cross), axis=1, keepdims=True)
        sums[tap(off, -1)] = jnp.sum(jnp.where(second, cross, 0.0), axis=1, keepdims=True)
    spot = lax.broadcasted_iota(jnp.int32, (SIZE, CH), 1)
    tap_sums = jnp.zeros((SIZE, CH), jnp.float32)
    for index in range(9):
        tap_sums = jnp.where(spot == index, sums[index], tap_sums)
    return out, d_values, tap_sums


def kernel(
    x_ref, g_ref, qkv_ref, proj_ref, lepe_ref,
    gf_out, qkv_out, proj_out, lepe_out,
    w_tra, taps, sent, arrived, back, returned, pair, nat, tra, out_s, dq_s, dk_s, dv_s, unit_h, acc, tap_acc,
    parts_h, plane_h, depth_h, total_h, parts_v, plane_v, depth_v, total_v, unit_s, inv_s,
    send_f, recv_f, send_r, recv_r, send_a, recv_a, send_b, recv_b, send_c, recv_c,
):
    row = lax.axis_index("rows")
    batch = lax.axis_index("batch")
    core = row % 2
    z_high = (row // 2) % 4
    mine = (row // 8) * 2 + core
    level = z_high * 2 + batch

    def plane_peer(other):
        return ((other // 2) * 8 + z_high * 2 + other % 2, batch)

    def depth_peer(other):
        return ((row // 8) * 8 + (other // 2) * 2 + core, other % 2)

    barrier = pltpu.get_barrier_semaphore()

    @pl.loop(1, OWNERS)
    def _(step):
        pl.semaphore_signal(barrier, inc=1, device_id=((row + step) % OWNERS, batch), device_id_type=MESH)

    @pl.loop(0, 4)
    def _(step):
        pl.semaphore_signal(barrier, inc=1, device_id=depth_peer(step * 2 + 1 - batch), device_id_type=MESH)

    out_row = lax.broadcasted_iota(jnp.int32, (256, 256), 0)
    in_row = lax.broadcasted_iota(jnp.int32, (256, 256), 1)
    source_row = ((out_row // 2) % 4) * PIECE + ((out_row // 8) % 16) * 4 + (out_row // 128) * 2 + out_row % 2
    permute = (in_row == source_row).astype(jnp.float32).astype(jnp.bfloat16)
    for q in range(WIDTH // PIECE):
        both = jnp.concatenate(
            [
                jnp.concatenate(
                    [ref[r * WIDTH + q * PIECE : r * WIDTH + (q + 1) * PIECE, :] for r in range(BAND)], axis=0
                )
                for ref in (x_ref, g_ref)
            ],
            axis=1,
        )
        packed = dot(permute, both).reshape(2, 16, 8, 2 * CH).astype(jnp.bfloat16)
        sent[0, q * 16 : (q + 1) * 16] = packed[0]
        sent[1, q * 16 : (q + 1) * 16] = packed[1]

    qkv_tra = qkv_ref[...].astype(jnp.float32).T
    for head in range(NUM_HEADS):
        rows = [qkv_tra[part * CH + head * SIZE : part * CH + (head + 1) * SIZE, :] for part in range(3)]
        rows.append(jnp.zeros((SIZE, CH), jnp.float32))
        w_tra[head, :, :CH] = jnp.concatenate(rows, axis=0).astype(jnp.bfloat16)
        w_tra[head, : 3 * SIZE, CH:] = jnp.zeros((3 * SIZE, CH), jnp.bfloat16)
        w_tra[head, 3 * SIZE :, CH:] = proj_ref[head * SIZE : (head + 1) * SIZE, :]
    taps[...] = jnp.concatenate([lepe_ref[...].astype(jnp.float32), jnp.zeros((7, CH), jnp.float32)], axis=0).T
    acc[...] = jnp.zeros_like(acc)
    tap_acc[...] = jnp.zeros_like(tap_acc)

    pl.semaphore_wait(barrier, OWNERS - 1 + 4)

    def forward(stripe, other, slot):
        return pltpu.make_async_remote_copy(
            src_ref=sent.at[stripe, other], dst_ref=arrived.at[stripe, slot],
            send_sem=send_f.at[stripe], recv_sem=recv_f.at[stripe],
            device_id=(other, batch), device_id_type=MESH,
        )

    def backward(stripe, head, other, slot):
        return pltpu.make_async_remote_copy(
            src_ref=back.at[stripe, head, other], dst_ref=returned.at[stripe, head, slot],
            send_sem=send_r.at[stripe, head], recv_sem=recv_r.at[stripe, head],
            device_id=(other, batch), device_id_type=MESH,
        )

    def all_forward(stripe):
        return pltpu.make_async_remote_copy(
            src_ref=sent.at[stripe, pl.ds(0, OWNERS - 1)], dst_ref=arrived.at[stripe, pl.ds(0, OWNERS - 1)],
            send_sem=send_f.at[stripe], recv_sem=recv_f.at[stripe],
            device_id=((row + 1) % OWNERS, batch), device_id_type=MESH,
        )

    def all_backward(stripe, head):
        return pltpu.make_async_remote_copy(
            src_ref=back.at[stripe, head, pl.ds(0, OWNERS - 1)], dst_ref=returned.at[stripe, head, pl.ds(0, OWNERS - 1)],
            send_sem=send_r.at[stripe, head], recv_sem=recv_r.at[stripe, head],
            device_id=((row + 1) % OWNERS, batch), device_id_type=MESH,
        )

    bufs = ((parts_h, plane_h, depth_h, total_h), (parts_v, plane_v, depth_v, total_v))

    def copy_a(side, other, slot):
        return pltpu.make_async_remote_copy(
            src_ref=bufs[side][0].at[other], dst_ref=bufs[side][1].at[slot],
            send_sem=send_a.at[side, other], recv_sem=recv_a.at[side, slot],
            device_id=plane_peer(other), device_id_type=MESH,
        )

    def copy_b(side, other, slot):
        return pltpu.make_async_remote_copy(
            src_ref=bufs[side][2].at[level], dst_ref=bufs[side][2].at[slot],
            send_sem=send_b.at[side, other], recv_sem=recv_b.at[side, slot],
            device_id=depth_peer(other), device_id_type=MESH,
        )

    def copy_c(side, other, slot):
        return pltpu.make_async_remote_copy(
            src_ref=bufs[side][3].at[mine], dst_ref=bufs[side][3].at[slot],
            send_sem=send_c.at[side, other], recv_sem=recv_c.at[side, slot],
            device_id=plane_peer(other), device_id_type=MESH,
        )

    def start_a(side):
        parts, plane = bufs[side][:2]
        for index in range(PLANE):
            head, place = 2 * side + index // 16, index % 16
            parts[index, :8, :] = acc[head, place * 8 : (place + 1) * 8, :]
        if side == 1:
            tap_rows = tap_acc[...].T
            for index in range(9):
                parts[index, 8:, :] = tap_rows[index : index + 1, :]
            for index in range(9, PLANE):
                parts[index, 8:, :] = jnp.zeros((1, CH), jnp.float32)

        @pl.loop(1, PLANE)
        def _(step):
            copy_a(side, (mine + step) % PLANE, mine).start()

        plane[mine] = parts[mine]

    def start_b(side):
        _, plane, depth, _ = bufs[side]

        @pl.loop(1, PLANE)
        def _(step):
            other = (mine + step) % PLANE
            copy_a(side, other, other).wait_recv()

        sums = [plane[index] for index in range(PLANE)]
        while len(sums) > 1:
            sums = [one + two for one, two in zip(sums[::2], sums[1::2])]
        depth[level] = sums[0]

        @pl.loop(1, DEPTH)
        def _(step):
            copy_b(side, (level + step) % DEPTH, level).start()

    def start_c(side):
        _, _, depth, total = bufs[side]

        @pl.loop(1, DEPTH)
        def _(step):
            other = (level + step) % DEPTH
            copy_b(side, other, other).wait_recv()

        sums = [depth[index] for index in range(DEPTH)]
        while len(sums) > 1:
            sums = [one + two for one, two in zip(sums[::2], sums[1::2])]
        total[mine] = sums[0]

        @pl.loop(1, PLANE)
        def _(step):
            copy_c(side, (mine + step) % PLANE, mine).start()

    for stripe in range(2):

        @pl.loop(1, OWNERS)
        def _(step):
            forward(stripe, (row + step) % OWNERS, row).start()

    for stripe in range(2):
        arrived[stripe, row] = sent[stripe, row]

    def one_head(head, vertical):
        nat[...] = dot(pair[...], w_tra[head], COLS).astype(jnp.bfloat16)
        tra[...] = dot(w_tra[head], pair[...], COLS).astype(jnp.bfloat16)
        attention(nat, tra, out_s, dq_s, dk_s, dv_s)
        values = tra[2 * SIZE : 3 * SIZE, :].astype(jnp.float32)
        lifted = tra[3 * SIZE :, :].astype(jnp.float32)
        channels = slice(head * SIZE, (head + 1) * SIZE)
        near_out, near_dv, tap_sums = lepe(values, lifted, taps[channels, :], vertical)
        whole = jnp.concatenate(
            [
                dq_s[...].astype(jnp.bfloat16),
                dk_s[...].astype(jnp.bfloat16),
                (dv_s[...] + near_dv).astype(jnp.bfloat16),
                (out_s[...] + near_out).astype(jnp.bfloat16),
            ],
            axis=0,
        )
        tap_acc[channels, :] += tap_sums
        part = dot(whole, pair[...])
        acc[head, : 3 * SIZE, :] += part[: 3 * SIZE, :CH]
        acc[head, 3 * SIZE :, :] += part[3 * SIZE :, CH:]
        return whole

    @pl.loop(0, 2)
    def _(turn):
        base = pl.multiple_of(turn * LEN, LEN)
        unit, _ = normalise(x_ref[pl.ds(base, LEN), :].astype(jnp.float32))
        pair[:, :CH] = unit.astype(jnp.bfloat16)
        pair[:, CH:] = g_ref[pl.ds(base, LEN), :]
        for head in range(2):
            whole = one_head(head, False)
            share = dot(whole, w_tra[head, :, :CH], ROWS)
            if head == 0:
                unit_h[pl.ds(base, LEN), :] = share
            else:
                unit_h[pl.ds(base, LEN), :] += share

    start_a(0)

    @pl.loop(0, 2)
    def _(turn):
        all_forward(turn).wait_recv()
        unit, _ = normalise(arrived[turn, :, :, :CH].astype(jnp.float32).reshape(LEN, CH))
        pair[:, :CH] = unit.astype(jnp.bfloat16)
        pair[:, CH:] = arrived[turn, :, :, CH:].astype(jnp.float32).reshape(LEN, CH).astype(jnp.bfloat16)
        for head in range(2):
            whole = one_head(2 + head, True)
            if head == 1:

                @pl.when(turn == 1)
                def _():
                    start_a(1)

            back[turn, head] = whole.astype(jnp.float32).T.reshape(OWNERS, 8, CH).astype(jnp.bfloat16)

            @pl.loop(1, OWNERS)
            def _(step):
                backward(turn, head, (row + step) % OWNERS, row).start()

            returned[turn, head, row] = back[turn, head, row]

        @pl.when(turn == 0)
        def _():
            start_b(0)

    start_c(0)
    for index in range((BAND * WIDTH) // 256):
        place = slice(index * 256, (index + 1) * 256)
        unit, inv_std = normalise(x_ref[place, :].astype(jnp.float32))
        unit_s[place, :] = unit
        inv_s[place, :] = jnp.broadcast_to(inv_std, (256, CH))
    start_b(1)
    start_c(1)

    for stripe in range(2):
        for head in range(2):
            all_backward(stripe, head).wait_recv()

    @pl.loop(0, WIDTH // PIECE)
    def _(q):
        owners = pl.ds(q * 16, 16)
        grads = jnp.concatenate(
            [
                jnp.concatenate(
                    [returned[j, head, owners].astype(jnp.float32).reshape(128, CH) for j in range(2)], axis=0
                ).astype(jnp.bfloat16)
                for head in range(2)
            ],
            axis=1,
        )
        ordered = dot(permute, grads, ROWS).astype(jnp.bfloat16)
        weights = jnp.concatenate([w_tra[2, :, :CH], w_tra[3, :, :CH]], axis=0)
        grad_v = dot(ordered, weights)
        for r in range(BAND):
            place = pl.ds(pl.multiple_of(r * WIDTH + q * PIECE, PIECE), PIECE)
            unit, inv_std = unit_s[place, :], inv_s[place, :]
            grad_unit = unit_h[place, :] + grad_v[r * PIECE : (r + 1) * PIECE, :]
            mean = jnp.mean(grad_unit, axis=1, keepdims=True)
            along = jnp.mean(grad_unit * unit, axis=1, keepdims=True)
            grad_norm = (grad_unit - mean - unit * along) * inv_std
            gf_out[place, :] = (g_ref[place, :].astype(jnp.float32) + grad_norm).astype(jnp.bfloat16)

    for side in range(2):

        @pl.loop(1, PLANE)
        def _(step):
            other = (mine + step) % PLANE
            copy_c(side, other, other).wait_recv()

    z = (2 * 512 * 512) ** (-0.5)

    def rows_of(head, start):
        total = bufs[head // 2][3]
        return [total[(head % 2) * 16 + start // 8 + part, :8, :] for part in range(SIZE // 8)]

    for part in range(3):
        pieces = [piece for head in range(NUM_HEADS) for piece in rows_of(head, part * SIZE)]
        qkv_out[:, part * CH : (part + 1) * CH] = jnp.concatenate(pieces, axis=0).T * z
    proj_out[...] = jnp.concatenate([piece for head in range(NUM_HEADS) for piece in rows_of(head, 3 * SIZE)], axis=0) * z
    lepe_out[...] = jnp.concatenate([total_v[index, 8:, :] for index in range(9)], axis=0) * z

    for stripe in range(2):
        all_forward(stripe).wait_send()
        for head in range(2):
            all_backward(stripe, head).wait_send()

    for side in range(2):

        @pl.loop(1, PLANE)
        def _(step):
            other = (mine + step) % PLANE
            copy_a(side, other, mine).wait_send()
            copy_c(side, other, mine).wait_send()

        @pl.loop(1, DEPTH)
        def _(step):
            copy_b(side, (level + step) % DEPTH, level).wait_send()


def hand_over(*refs):
    for source, target in zip(refs[:4], refs[4:]):
        target[...] = source[...]


def body(features, grad_out, qkv_weight, proj_weight, lepe_weight):
    tokens = BAND * WIDTH
    vmem = pl.BlockSpec(memory_space=pltpu.VMEM)
    low, wide = jnp.bfloat16, jnp.float32
    dma = pltpu.SemaphoreType.DMA
    grad_features, grad_qkv, grad_proj, grad_lepe = pl.pallas_call(
        kernel,
        in_specs=[vmem] * 5,
        out_specs=[vmem] * 4,
        out_shape=[
            jax.ShapeDtypeStruct((tokens, CH), low),
            jax.ShapeDtypeStruct((CH, 3 * CH), wide),
            jax.ShapeDtypeStruct((CH, CH), wide),
            jax.ShapeDtypeStruct((9, CH), wide),
        ],
        scratch_shapes=[
            pltpu.VMEM((NUM_HEADS, CH, 2 * CH), low),
            pltpu.VMEM((CH, 16), wide),
            pltpu.VMEM((2, OWNERS, 8, 2 * CH), low),
            pltpu.VMEM((2, OWNERS, 8, 2 * CH), low),
            pltpu.VMEM((2, 2, OWNERS, 8, CH), low),
            pltpu.VMEM((2, 2, OWNERS, 8, CH), low),
            pltpu.VMEM((LEN, 2 * CH), low),
            pltpu.VMEM((LEN, CH), low),
            pltpu.VMEM((CH, LEN), low),
            pltpu.VMEM((SIZE, LEN), wide),
            pltpu.VMEM((SIZE, LEN), wide),
            pltpu.VMEM((SIZE, LEN), wide),
            pltpu.VMEM((SIZE, LEN), wide),
            pltpu.VMEM((tokens, CH), wide),
            pltpu.VMEM((NUM_HEADS, CH, CH), wide),
            pltpu.VMEM((CH, CH), wide),
            pltpu.VMEM((PLANE, 8, CH), wide),
            pltpu.VMEM((PLANE, 8, CH), wide),
            pltpu.VMEM((DEPTH, 8, CH), wide),
            pltpu.VMEM((PLANE, 8, CH), wide),
            pltpu.VMEM((PLANE, 9, CH), wide),
            pltpu.VMEM((PLANE, 9, CH), wide),
            pltpu.VMEM((DEPTH, 9, CH), wide),
            pltpu.VMEM((PLANE, 9, CH), wide),
            pltpu.VMEM((tokens, CH), wide),
            pltpu.VMEM((tokens, CH), wide),
            dma((2,)), dma((2,)), dma((2, 2)), dma((2, 2)),
            dma((2, PLANE)), dma((2, PLANE)), dma((2, DEPTH)), dma((2, DEPTH)), dma((2, PLANE)), dma((2, PLANE)),
        ],
        compiler_params=pltpu.CompilerParams(
            collective_id=0, has_side_effects=True, vmem_limit_bytes=60 << 20
        ),
    )(features.reshape(tokens, CH), grad_out.reshape(tokens, CH), qkv_weight, proj_weight, lepe_weight)
    results = pl.pallas_call(
        hand_over,
        in_specs=[vmem] * 4,
        out_specs=[vmem] * 4,
        out_shape=[jax.ShapeDtypeStruct(a.shape, a.dtype) for a in (grad_features, grad_qkv, grad_proj, grad_lepe)],
    )(grad_features, grad_qkv, grad_proj, grad_lepe)
    return (results[0].reshape(features.shape), *results[1:])


def solution(mesh):
    in_specs = (P("batch", "rows", None, None), P("batch", "rows", None, None), P(), P(), P())
    out_specs = (P("batch", "rows", None, None), P(), P(), P())
    return jax.shard_map(body, mesh=mesh, in_specs=in_specs, out_specs=out_specs, check_vma=False)
```
